32 devices in a mesh: gx: 8 (over y, x, core), gy: 4 (over z).
Axes of the slice: x: 2, y: 2, z: 4, core: 2. Of those that a mesh axis runs over, the one named last changes fastest.
Arguments:
- probe_signs: int32 [32, 16, 64, 128], P(None, 'gx', 'gy'), may hold values from 0 to 1
- diagonal: float32 [16, 64, 128], P('gx', 'gy'), may hold values from 0.25 to 4
Outputs:
- diagonal_blocks: float32 [3, 32, 32], replicated
- offdiag_blocks: float32 [3, 32, 32], replicated
- next_block: float32 [32, 16, 64, 128], P(None, 'gx', 'gy')
The draws below stay inside these ranges and needn't reach their ends.
All inputs are finite; a program needn't handle non-finite values.
Results may differ from the reference program's by a relative error of at most 0.0006.
Values sent between devices are 32-bit elements; how exact they have to be, the bound alone decides.
A program may use at most 64 MiB of HBM per device.

```python
import math
import jax
import jax.numpy as jnp
from jax import lax

PROBES = 32
ITERS = 3
NX = 16
NY = 64
NZ = 128


def draw_probe_signs(key, part):
    common_bits = jax.random.randint(jax.random.fold_in(key, 11), (1, NX, NY, NZ), 0, 2)
    flip_limits = jax.random.randint(jax.random.fold_in(key, 12), (PROBES, 1, 1, 1), 15, 36)
    percent_draws = jax.random.randint(jax.random.fold_in(key, 13), (PROBES, NX, NY, NZ), 0, 100)
    flipped = (percent_draws < flip_limits).astype(jnp.int32)
    return ((common_bits + flipped) % 2).astype(jnp.int32)


def block_scale(own_key, extent, split, low, top_value):
    level, own = 1.0, jax.random.fold_in(own_key, 6)
    for dim, blocks in split:
        steps = jnp.exp(jax.random.uniform(jax.random.fold_in(own, dim), (blocks,), jnp.float32, low / len(split), top_value / len(split)))
        level = level * jnp.repeat(steps, extent[dim] // blocks).reshape([-1 if axis == dim else 1 for axis in range(len(extent))])
    return level


def setup_inputs(seed: int = 0) -> dict:
    keys = jax.random.split(jax.random.key(seed), 3)
    return {
        "probe_signs": draw_probe_signs(jax.random.fold_in(keys[2], 71), 0),
        "diagonal": jnp.clip(jnp.exp(math.log(4.0) - 2.7725887 * jax.random.uniform(keys[1], (NX, NY, NZ), jnp.float32) ** block_scale(keys[1], (NX, NY, NZ), ((0, 8), (1, 4)), -0.2, 0.2)), 0.25, 4.0),
    }


def stencil(vectors, diagonal):
    beside = jnp.roll(vectors, 1, 1) + jnp.roll(vectors, -1, 1)
    beside = beside + jnp.roll(vectors, 1, 2) + jnp.roll(vectors, -1, 2)
    beside = beside + jnp.roll(vectors, 1, 3) + jnp.roll(vectors, -1, 3)
    return (6.0 + diagonal)[None] * vectors - beside

def inner_block(left, right):
    return jnp.einsum('pxyz,qxyz->pq', left, right, precision=lax.Precision.HIGHEST)

def combine(vectors, matrix):
    return jnp.einsum('pxyz,pq->qxyz', vectors, matrix, precision=lax.Precision.HIGHEST)

def inverse_lower(gram_matrix):
    lower_factor = jnp.linalg.cholesky(gram_matrix)
    identity_matrix = jnp.eye(gram_matrix.shape[0], dtype=gram_matrix.dtype)
    inverse = lax.linalg.triangular_solve(lower_factor, identity_matrix, left_side=True, lower=True)
    return (lower_factor, inverse)

def reference(probe_signs, diagonal):
    scale_factor = 1.0 / jnp.sqrt(jnp.float32(NX * NY * NZ))
    probes = (2.0 * probe_signs.astype(jnp.float32) - 1.0) * scale_factor
    lower_factor, inverse = inverse_lower(inner_block(probes, probes))
    current = combine(probes, inverse.T)
    previous = None
    coupling = None
    alphas = []
    betas = []
    for iteration in range(ITERS):
        image = stencil(current, diagonal)
        if previous is not None:
            image = image - combine(previous, coupling)
        projected = inner_block(current, image)
        remain = image - combine(current, projected)
        lower_factor, inverse = inverse_lower(inner_block(remain, remain))
        alphas.append(projected)
        betas.append(lower_factor.T)
        previous = current
        coupling = lower_factor
        current = combine(remain, inverse.T)
    return (jnp.stack(alphas), jnp.stack(betas), current)
```

```python
import functools

import jax
import jax.numpy as jnp
from jax import lax
from jax.experimental import pallas as pl
from jax.experimental.pallas import tpu as pltpu
from jax.sharding import PartitionSpec as P

ITERS = 3
CHUNK = 8
CENTRE = 7.5
SCALE = 2.5
PANEL = 4
MESH = pl.DeviceIdType.MESH


def mm(left, right, left_dim=1, right_dim=0):
    return lax.dot_general(
        left,
        right,
        (((left_dim,), (right_dim,)), ((), ())),
        precision=lax.Precision.HIGHEST,
        preferred_element_type=jnp.float32,
    )


def factor(matrix):
    size = matrix.shape[0]
    rows = lax.broadcasted_iota(jnp.int32, (size, size), 0)
    columns = lax.broadcasted_iota(jnp.int32, (size, size), 1)
    upper = matrix
    inverse = jnp.where(rows == columns, 1.0, 0.0).astype(jnp.float32)
    for start in range(0, size, PANEL):
        panel = [
            jnp.broadcast_to(upper[:, start + m : start + m + 1], (size, size)) for m in range(PANEL)
        ]
        for m in range(PANEL):
            at = start + m
            pivot = panel[m][at : at + 1, :]
            root = lax.rsqrt(pivot)
            root = root * (1.5 - 0.5 * pivot * root * root)
            below = jnp.where(rows > at, panel[m] * root, 0.0)
            upper_row = upper[at : at + 1, :] * root
            inverse_row = inverse[at : at + 1, :] * root
            upper = jnp.where(rows == at, upper_row, upper - below * upper_row)
            inverse = jnp.where(rows == at, inverse_row, inverse - below * inverse_row)
            for later in range(m + 1, PANEL):
                panel[later] = panel[later] - below * below[start + later : start + later + 1, :]
    return jnp.where(columns >= rows, upper, 0.0), inverse


def kernel(
    nx, ny, probes_ref, diagonal_ref, alphas_ref, betas_ref, next_ref,
    fields, split, moments, part_x, part_y, total,
    send_halo, recv_halo, send_sum, recv_sum, send_z, recv_z, send_all, recv_all,
):
    chunks, planes, lines = probes_ref.shape[0], probes_ref.shape[1], probes_ref.shape[2]
    probes = chunks * CHUNK
    gx, gy = lax.axis_index("gx"), lax.axis_index("gy")

    def x_device(offset):
        return lax.rem(gx + offset, nx)

    def y_device(offset):
        return lax.rem(gy + offset, ny)

    barrier = pltpu.get_barrier_semaphore()
    for offset in range(1, nx):
        pl.semaphore_signal(barrier, inc=1, device_id={"gx": x_device(offset)}, device_id_type=MESH)
    for offset in range(1, ny):
        pl.semaphore_signal(barrier, inc=1, device_id={"gy": y_device(offset)}, device_id_type=MESH)
    pl.semaphore_wait(barrier, nx + ny - 2)

    inner_x, inner_y = pl.ds(1, planes), pl.ds(1, lines)

    def halo_copies(step):
        here = fields.at[step]
        moves = (
            (here.at[planes, inner_y], here.at[0, inner_y], {"gx": x_device(1)}),
            (here.at[1, inner_y], here.at[planes + 1, inner_y], {"gx": x_device(nx - 1)}),
            (here.at[inner_x, lines], here.at[inner_x, 0], {"gy": y_device(1)}),
            (here.at[inner_x, 1], here.at[inner_x, lines + 1], {"gy": y_device(ny - 1)}),
        )
        return [
            pltpu.make_async_remote_copy(
                src_ref=source,
                dst_ref=target,
                send_sem=send_halo.at[step, side],
                recv_sem=recv_halo.at[step, side],
                device_id=device,
                device_id_type=MESH,
            )
            for side, (source, target, device) in enumerate(moves)
        ]

    def load_chunk(chunk, carry):
        for x in range(planes):
            for y in range(lines):
                fields[chunk, x + 1, y + 1] = probes_ref[chunk, x, y]
        for copy in halo_copies(chunk):
            copy.start()
        return carry

    lax.fori_loop(0, chunks, load_chunk, 0)

    def split_level(level):
        for x in range(planes):
            for y in range(lines):
                value = jnp.concatenate(
                    [fields[level * chunks + c, x + 1, y + 1] for c in range(chunks)], axis=0
                )
                high = value.astype(jnp.bfloat16)
                low = (value - high.astype(jnp.float32)).astype(jnp.bfloat16)
                lanes = pl.ds((x * lines + y) * value.shape[1], value.shape[1])
                split[level, 0:probes, lanes] = high
                split[level, probes : 2 * probes, lanes] = low

    def gram(left, right):
        product = lax.dot_general(
            split[left], split[right], (((1,), (1,)), ((), ())), preferred_element_type=jnp.float32
        )
        return (
            (product[probes:, probes:] + (product[:probes, probes:] + product[probes:, :probes]))
            + product[:probes, :probes]
        )

    grams = []
    for level in range(ITERS):

        def apply_chunk(chunk, carry, level=level):
            step = level * chunks + chunk
            for copy in halo_copies(step):
                copy.wait_recv()
            for x in range(1, planes + 1):
                for y in range(1, lines + 1):
                    value = fields[step, x, y]
                    beside = fields[step, x - 1, y] + fields[step, x + 1, y]
                    beside = beside + (fields[step, x, y - 1] + fields[step, x, y + 1])
                    beside = beside + (
                        pltpu.roll(value, 1, 1) + pltpu.roll(value, value.shape[1] - 1, 1)
                    )
                    own = jnp.broadcast_to(diagonal_ref[x - 1, y - 1 : y, :], value.shape)
                    fields[step + chunks, x, y] = own * value - beside * (1.0 / SCALE)
            if level + 1 < ITERS:
                for copy in halo_copies(step + chunks):
                    copy.start()
            return carry

        if level == 0:
            split_level(0)
            grams.append(gram(0, 0))
        lax.fori_loop(0, chunks, apply_chunk, 0)
        split_level(level + 1)
        grams.append(gram(level, level + 1))
        grams.append(gram(level + 1, level + 1))

    zero = jnp.zeros_like(grams[0])
    width = moments.shape[1]
    per_row = width // probes
    grams_padded = grams + [zero] * (-len(grams) % per_row)
    bands = len(grams_padded) // per_row
    for band in range(bands):
        moments[band * probes : (band + 1) * probes, :] = jnp.concatenate(
            grams_padded[band * per_row : (band + 1) * per_row], axis=1
        )
    piece = moments.shape[0] // nx
    if moments.shape[0] > bands * probes:
        moments[bands * probes :, :] = jnp.zeros_like(moments[bands * probes :, :])

    def rows_of(index):
        return pl.ds(pl.multiple_of(index * piece, piece), piece)

    copies = []
    for offset in range(1, nx):
        copies.append(
            pltpu.make_async_remote_copy(
                src_ref=moments.at[rows_of(x_device(offset))],
                dst_ref=part_x.at[offset],
                send_sem=send_sum.at[offset],
                recv_sem=recv_sum.at[offset],
                device_id={"gx": x_device(offset)},
                device_id_type=MESH,
            )
        )
        copies[-1].start()
    partial = moments[rows_of(gx), :]
    for offset in range(1, nx):
        copies[offset - 1].wait_recv()
        partial = partial + part_x[offset]
    part_y[gy] = partial
    copies_y = []
    for offset in range(1, ny):
        copies_y.append(
            pltpu.make_async_remote_copy(
                src_ref=part_y.at[gy],
                dst_ref=part_y.at[gy],
                send_sem=send_z.at[offset],
                recv_sem=recv_z.at[offset],
                device_id={"gy": y_device(offset)},
                device_id_type=MESH,
            )
        )
        copies_y[-1].start()
    for copy in copies_y:
        copy.wait_recv()
    whole = part_y[0]
    for index in range(1, ny):
        whole = whole + part_y[index]
    total[rows_of(gx), :] = whole
    copies_all = []
    for offset in range(1, nx):
        copies_all.append(
            pltpu.make_async_remote_copy(
                src_ref=total.at[rows_of(gx)],
                dst_ref=total.at[rows_of(gx)],
                send_sem=send_all.at[offset],
                recv_sem=recv_all.at[offset],
                device_id={"gx": x_device(offset)},
                device_id_type=MESH,
            )
        )
        copies_all[-1].start()
    for copy in copies_all:
        copy.wait_recv()

    moment = []
    for index in range(len(grams)):
        band, place = index // per_row, index % per_row
        block = total[band * probes : (band + 1) * probes, :]
        moment.append(block[:, place * probes : (place + 1) * probes])

    levels = ITERS + 1
    lower = {}
    uppers, inverses = [], []
    for j in range(levels):
        pivot = moment[2 * j]
        for i in range(j):
            pivot = pivot - mm(lower[j, i], lower[j, i], 1, 1)
        upper, inverse = factor(pivot)
        uppers.append(upper)
        inverses.append(inverse)
        for k in range(j + 1, levels):
            rest = moment[j + k]
            for i in range(j):
                rest = rest - mm(lower[k, i], lower[j, i], 1, 1)
            lower[k, j] = mm(rest, inverse, 1, 1)

    rows = lax.broadcasted_iota(jnp.int32, (probes, probes), 0)
    columns = lax.broadcasted_iota(jnp.int32, (probes, probes), 1)
    shift = jnp.where(rows == columns, CENTRE, 0.0).astype(jnp.float32)
    before = None
    for j in range(ITERS):
        inside = lower[j + 1, j]
        if before is not None:
            inside = inside - mm(lower[j, j - 1], before, 1, 1)
        alphas_ref[j] = shift + SCALE * mm(inverses[j], inside)
        before = mm(uppers[j + 1], inverses[j], 1, 1)
        betas_ref[j] = SCALE * before

    mixing = [None] * levels
    mixing[ITERS] = inverses[ITERS]
    for k in range(ITERS - 1, -1, -1):
        gathered = mm(mixing[ITERS], lower[ITERS, k])
        for i in range(k + 1, ITERS):
            gathered = gathered + mm(mixing[i], lower[i, k])
        mixing[k] = -mm(gathered, inverses[k])
    pieces = []
    for block in mixing:
        high = block.astype(jnp.bfloat16)
        pieces.append((high, (block - high.astype(jnp.float32)).astype(jnp.bfloat16)))
    weights = jnp.concatenate(
        [jnp.concatenate([part[side] for part in pieces for _ in range(2)], axis=1) for side in range(2)],
        axis=0,
    )
    lanes = next_ref.shape[2]
    group = 4
    basis = split.at[...].reshape(levels * 2 * probes, split.shape[2])
    for start in range(0, planes * lines, group):
        product = jnp.dot(
            weights,
            basis[:, start * lanes : (start + group) * lanes],
            preferred_element_type=jnp.float32,
        )
        product = product[:probes] + product[probes:]
        for inner in range(group):
            next_ref[start + inner] = product[:, inner * lanes : (inner + 1) * lanes]

    def finish(step, carry):
        for copy in halo_copies(step):
            copy.wait_send()
        return carry

    lax.fori_loop(0, ITERS * chunks, finish, 0)
    for copy in copies + copies_y + copies_all:
        copy.wait_send()


def per_device(nx, ny, probe_signs, diagonal):
    probes, planes, lines, lanes = probe_signs.shape
    chunks = probes // CHUNK
    signs = 2.0 * probe_signs.astype(jnp.float32) - 1.0
    signs = signs.reshape(chunks, CHUNK, planes, lines, lanes).transpose(0, 2, 3, 1, 4)
    own = (6.0 - CENTRE + diagonal) * (1.0 / SCALE)
    levels = ITERS + 1
    bands = -(-(2 * ITERS + 1) * probes // lanes)
    rows = max(bands * probes, 8 * nx)
    piece = rows // nx
    small = jax.ShapeDtypeStruct((ITERS, probes, probes), jnp.float32)
    vmem = pl.BlockSpec(memory_space=pltpu.VMEM)
    dma = pltpu.SemaphoreType.DMA
    alphas, betas, block = pl.pallas_call(
        functools.partial(kernel, nx, ny),
        out_shape=(
            small,
            small,
            jax.ShapeDtypeStruct((planes * lines, probes, lanes), jnp.float32),
        ),
        in_specs=[vmem, vmem],
        out_specs=(vmem, vmem, vmem),
        scratch_shapes=[
            pltpu.VMEM((levels * chunks, planes + 2, lines + 2, CHUNK, lanes), jnp.float32),
            pltpu.VMEM((levels, 2 * probes, planes * lines * lanes), jnp.bfloat16),
            pltpu.VMEM((rows, lanes), jnp.float32),
            pltpu.VMEM((nx, piece, lanes), jnp.float32),
            pltpu.VMEM((ny, piece, lanes), jnp.float32),
            pltpu.VMEM((rows, lanes), jnp.float32),
            dma((ITERS * chunks, 4)),
            dma((ITERS * chunks, 4)),
            dma((nx,)),
            dma((nx,)),
            dma((ny,)),
            dma((ny,)),
            dma((nx,)),
            dma((nx,)),
        ],
        compiler_params=pltpu.CompilerParams(collective_id=0, has_side_effects=True),
        name="lanczos",
    )(signs, own)
    block = block.reshape(planes, lines, probes, lanes).transpose(2, 0, 1, 3)
    return alphas, betas, block


def solution(mesh):
    nx, ny = mesh.shape["gx"], mesh.shape["gy"]
    in_specs = (P(None, "gx", "gy", None), P("gx", "gy", None))
    out_specs = (P(), P(), P(None, "gx", "gy", None))
    return jax.shard_map(
        functools.partial(per_device, nx, ny),
        mesh=mesh,
        in_specs=in_specs,
        out_specs=out_specs,
        check_vma=False,
    )
```

```python
import functools

import jax
import jax.numpy as jnp
from jax import lax
from jax.experimental import pallas as pl
from jax.experimental.pallas import tpu as pltpu
from jax.sharding import PartitionSpec as P

ITERS = 3
CHUNK = 8
CENTRE = 7.5
SCALE = 2.5
PANEL = 4
VMEM_BYTES = 24 * 1024 * 1024
MESH = pl.DeviceIdType.MESH


def mm(left, right, left_dim=1, right_dim=0):
    return lax.dot_general(
        left,
        right,
        (((left_dim,), (right_dim,)), ((), ())),
        precision=lax.Precision.HIGHEST,
        preferred_element_type=jnp.float32,
    )


def factor(matrix):
    size = matrix.shape[0]
    rows = lax.broadcasted_iota(jnp.int32, (size, size), 0)
    columns = lax.broadcasted_iota(jnp.int32, (size, size), 1)
    upper = matrix
    inverse = jnp.where(rows == columns, 1.0, 0.0).astype(jnp.float32)
    for start in range(0, size, PANEL):
        panel = [
            jnp.broadcast_to(upper[:, start + m : start + m + 1], (size, size)) for m in range(PANEL)
        ]
        for m in range(PANEL):
            at = start + m
            pivot = panel[m][at : at + 1, :]
            root = lax.rsqrt(pivot)
            root = root * (1.5 - 0.5 * pivot * root * root)
            below = jnp.where(rows > at, panel[m] * root, 0.0)
            upper_row = upper[at : at + 1, :] * root
            inverse_row = inverse[at : at + 1, :] * root
            upper = jnp.where(rows == at, upper_row, upper - below * upper_row)
            inverse = jnp.where(rows == at, inverse_row, inverse - below * inverse_row)
            for later in range(m + 1, PANEL):
                panel[later] = panel[later] - below * below[start + later : start + later + 1, :]
    return jnp.where(columns >= rows, upper, 0.0), inverse


def pack(matrix, lanes):
    per = lanes // matrix.shape[1]
    rows = matrix.shape[0] // per
    return jnp.concatenate([matrix[i * rows : (i + 1) * rows] for i in range(per)], axis=1)


def unpack(packed, size):
    per = packed.shape[1] // size
    return jnp.concatenate([packed[:, i * size : (i + 1) * size] for i in range(per)], axis=0)


def kernel(
    nx, ny, signs_ref, diagonal_ref, alphas_ref, betas_ref, next_ref,
    fields, split, part_x, part_y,
    send_halo, recv_halo, send_x, recv_x, send_y, recv_y,
):
    planes, lines, lanes = diagonal_ref.shape
    cells = planes * lines
    probes = signs_ref.shape[0] // cells
    chunks = probes // CHUNK
    gx, gy = lax.axis_index("gx"), lax.axis_index("gy")

    def x_device(offset):
        return lax.rem(gx + offset, nx)

    def y_device(offset):
        return lax.rem(gy + offset, ny)

    barrier = pltpu.get_barrier_semaphore()
    for offset in range(1, nx):
        pl.semaphore_signal(barrier, inc=1, device_id={"gx": x_device(offset)}, device_id_type=MESH)
    for offset in range(1, ny):
        pl.semaphore_signal(barrier, inc=1, device_id={"gy": y_device(offset)}, device_id_type=MESH)

    inner_x, inner_y = pl.ds(1, planes), pl.ds(1, lines)

    def halo_copies(step):
        here = fields.at[step]
        moves = (
            (here.at[planes, inner_y], here.at[0, inner_y], {"gx": x_device(1)}),
            (here.at[1, inner_y], here.at[planes + 1, inner_y], {"gx": x_device(nx - 1)}),
            (here.at[inner_x, lines], here.at[inner_x, 0], {"gy": y_device(1)}),
            (here.at[inner_x, 1], here.at[inner_x, lines + 1], {"gy": y_device(ny - 1)}),
        )
        return [
            pltpu.make_async_remote_copy(
                src_ref=source,
                dst_ref=target,
                send_sem=send_halo.at[step, side],
                recv_sem=recv_halo.at[step, side],
                device_id=device,
                device_id_type=MESH,
            )
            for side, (source, target, device) in enumerate(moves)
        ]

    def load_chunk(chunk):
        for x in range(planes):
            for y in range(lines):
                start = chunk * CHUNK * cells + x * lines + y
                bits = signs_ref[pl.ds(start, CHUNK, stride=cells), :]
                fields[chunk, x + 1, y + 1] = 2.0 * bits.astype(jnp.float32) - 1.0

    load_chunk(0)
    pl.semaphore_wait(barrier, nx + ny - 2)
    for chunk in range(chunks):
        if chunk > 0:
            load_chunk(chunk)
        for copy in halo_copies(chunk):
            copy.start()

    def split_level(level):
        for x in range(planes):
            for y in range(lines):
                value = jnp.concatenate(
                    [fields[level * chunks + c, x + 1, y + 1] for c in range(chunks)], axis=0
                )
                high = value.astype(jnp.bfloat16)
                low = (value - high.astype(jnp.float32)).astype(jnp.bfloat16)
                at = pl.ds((x * lines + y) * lanes, lanes)
                split[level, 0:probes, at] = high
                split[level, probes : 2 * probes, at] = low

    def gram(left, right):
        product = lax.dot_general(
            split[left], split[right], (((1,), (1,)), ((), ())), preferred_element_type=jnp.float32
        )
        return (
            (product[probes:, probes:] + (product[:probes, probes:] + product[probes:, :probes]))
            + product[:probes, :probes]
        )

    height = part_x.shape[2] // 2

    def along(group, count, offset, part, send, recv, me, device):
        rows = pl.ds(0, height * count)
        return pltpu.make_async_remote_copy(
            src_ref=part.at[group, me, rows],
            dst_ref=part.at[group, me, rows],
            send_sem=send.at[group, offset],
            recv_sem=recv.at[group, offset],
            device_id=device,
            device_id_type=MESH,
        )

    def x_copies(group, count):
        return [
            along(group, count, o, part_x, send_x, recv_x, gx, {"gx": x_device(o)})
            for o in range(1, nx)
        ]

    def y_copies(group, count):
        return [
            along(group, count, o, part_y, send_y, recv_y, gy, {"gy": y_device(o)})
            for o in range(1, ny)
        ]

    def begin(group, matrices):
        for i, matrix in enumerate(matrices):
            part_x[group, gx, i * height : (i + 1) * height] = pack(matrix, lanes)
        for copy in x_copies(group, len(matrices)):
            copy.start()

    def added(part, group, count, slots):
        value = part[group, 0, 0 : height * count]
        for slot in range(1, slots):
            value = value + part[group, slot, 0 : height * count]
        return value

    def middle(group, count):
        for copy in x_copies(group, count):
            copy.wait_recv()
        part_y[group, gy, 0 : height * count] = added(part_x, group, count, nx)
        for copy in y_copies(group, count):
            copy.start()

    def end(group, count):
        for copy in y_copies(group, count):
            copy.wait_recv()
        value = added(part_y, group, count, ny)
        return [unpack(value[i * height : (i + 1) * height], probes) for i in range(count)]

    def apply_level(level):
        def apply_chunk(chunk, carry):
            step = level * chunks + chunk
            for copy in halo_copies(step):
                copy.wait_recv()
            for x in range(1, planes + 1):
                for y in range(1, lines + 1):
                    value = fields[step, x, y]
                    beside = fields[step, x - 1, y] + fields[step, x + 1, y]
                    beside = beside + (fields[step, x, y - 1] + fields[step, x, y + 1])
                    beside = beside + (pltpu.roll(value, 1, 1) + pltpu.roll(value, lanes - 1, 1))
                    own = (diagonal_ref[x - 1, y - 1 : y, :] + (6.0 - CENTRE)) * (1.0 / SCALE)
                    fields[step + chunks, x, y] = (
                        jnp.broadcast_to(own, value.shape) * value - beside * (1.0 / SCALE)
                    )
            if level + 1 < ITERS:
                for copy in halo_copies(step + chunks):
                    copy.start()
            return carry

        lax.fori_loop(0, chunks, apply_chunk, 0)

    levels = ITERS + 1
    moment = []
    lower, inverse_of = {}, {}
    uppers, inverses, before = [], [], []
    rows = lax.broadcasted_iota(jnp.int32, (probes, probes), 0)
    columns = lax.broadcasted_iota(jnp.int32, (probes, probes), 1)
    shift = jnp.where(rows == columns, CENTRE, 0.0).astype(jnp.float32)

    def schur(k, j, matrix):
        for i in range(j):
            matrix = matrix - mm(lower[k, i], lower[j, i], 1, 1)
        return matrix

    def factor_level(j):
        upper, inverse = factor(schur(j, j, moment[2 * j]))
        uppers.append(upper)
        inverses.append(inverse)

    def link(k, j):
        lower[k, j] = mm(schur(k, j, moment[j + k]), inverses[j], 1, 1)

    def coefficients(j):
        inside = lower[j + 1, j]
        if j > 0:
            inside = inside - mm(lower[j, j - 1], before[j - 1], 1, 1)
        alphas_ref[j] = shift + SCALE * mm(inverses[j], inside)

    def coupling(j):
        before.append(mm(uppers[j + 1], inverses[j], 1, 1))
        betas_ref[j] = SCALE * before[j]

    def invert_row(j):
        inverse_of[j, j] = inverses[j]
        for k in range(j):
            gathered = mm(lower[j, k], inverse_of[k, k])
            for i in range(k + 1, j):
                gathered = gathered + mm(lower[j, i], inverse_of[i, k])
            inverse_of[j, k] = -mm(inverses[j], gathered)

    split_level(0)
    begin(0, [gram(0, 0)])
    apply_level(0)
    split_level(1)
    begin(1, [gram(0, 1), gram(1, 1)])
    middle(0, 1)
    apply_level(1)
    split_level(2)
    begin(2, [gram(1, 2), gram(2, 2)])
    middle(1, 2)
    moment.extend(end(0, 1))
    factor_level(0)
    apply_level(2)
    middle(2, 2)
    split_level(3)
    begin(3, [gram(2, 3), gram(3, 3)])
    moment.extend(end(1, 2))
    link(1, 0)
    link(2, 0)
    factor_level(1)
    coefficients(0)
    coupling(0)
    middle(3, 2)
    moment.extend(end(2, 2))
    link(3, 0)
    link(2, 1)
    link(3, 1)
    factor_level(2)
    coefficients(1)
    coupling(1)
    for j in range(3):
        invert_row(j)
    known = [
        mm(lower[3, 0], inverse_of[0, 0]) + mm(lower[3, 1], inverse_of[1, 0]),
        mm(lower[3, 1], inverse_of[1, 1]),
        None,
    ]
    moment.extend(end(3, 2))
    link(3, 2)
    factor_level(3)
    mixing = []
    for k in range(3):
        gathered = mm(lower[3, 2], inverse_of[2, k])
        if known[k] is not None:
            gathered = gathered + known[k]
        mixing.append(-mm(inverses[3], gathered))
    mixing.append(inverses[3])
    coefficients(2)
    coupling(2)

    pieces = []
    for block in mixing:
        high = block.astype(jnp.bfloat16)
        pieces.append((high, (block - high.astype(jnp.float32)).astype(jnp.bfloat16)))
    weights = jnp.concatenate(
        [jnp.concatenate([part[side] for part in pieces for _ in range(2)], axis=1) for side in range(2)],
        axis=0,
    )
    group = 4
    basis = split.at[...].reshape(levels * 2 * probes, split.shape[2])
    for start in range(0, cells, group):
        product = jnp.dot(
            weights,
            basis[:, start * lanes : (start + group) * lanes],
            preferred_element_type=jnp.float32,
        )
        product = product[:probes] + product[probes:]
        for inner in range(group):
            next_ref[pl.ds(start + inner, probes, stride=cells), :] = product[
                :, inner * lanes : (inner + 1) * lanes
            ]

    def finish(step, carry):
        for copy in halo_copies(step):
            copy.wait_send()
        return carry

    lax.fori_loop(0, ITERS * chunks, finish, 0)
    for index, count in enumerate((1, 2, 2, 2)):
        for copy in x_copies(index, count) + y_copies(index, count):
            copy.wait_send()


def per_device(nx, ny, probe_signs, diagonal):
    probes, planes, lines, lanes = probe_signs.shape
    chunks = probes // CHUNK
    levels = ITERS + 1
    height = probes * probes // lanes
    cells = planes * lines
    small = jax.ShapeDtypeStruct((ITERS, probes, probes), jnp.float32)
    vmem = pl.BlockSpec(memory_space=pltpu.VMEM)
    dma = pltpu.SemaphoreType.DMA
    alphas, betas, block = pl.pallas_call(
        functools.partial(kernel, nx, ny),
        out_shape=(small, small, jax.ShapeDtypeStruct((probes * cells, lanes), jnp.float32)),
        in_specs=[vmem, vmem],
        out_specs=(vmem, vmem, vmem),
        scratch_shapes=[
            pltpu.VMEM((levels * chunks, planes + 2, lines + 2, CHUNK, lanes), jnp.float32),
            pltpu.VMEM((levels, 2 * probes, cells * lanes), jnp.bfloat16),
            pltpu.VMEM((levels, nx, 2 * height, lanes), jnp.float32),
            pltpu.VMEM((levels, ny, 2 * height, lanes), jnp.float32),
            dma((ITERS * chunks, 4)),
            dma((ITERS * chunks, 4)),
            dma((levels, nx)),
            dma((levels, nx)),
            dma((levels, ny)),
            dma((levels, ny)),
        ],
        compiler_params=pltpu.CompilerParams(
            collective_id=0, has_side_effects=True, vmem_limit_bytes=VMEM_BYTES
        ),
        name="lanczos",
    )(probe_signs.reshape(probes * cells, lanes), diagonal)
    return alphas, betas, block.reshape(probes, planes, lines, lanes)


def solution(mesh):
    nx, ny = mesh.shape["gx"], mesh.shape["gy"]
    in_specs = (P(None, "gx", "gy", None), P("gx", "gy", None))
    out_specs = (P(), P(), P(None, "gx", "gy", None))
    return jax.shard_map(
        functools.partial(per_device, nx, ny),
        mesh=mesh,
        in_specs=in_specs,
        out_specs=out_specs,
        check_vma=False,
    )
```

```python
import functools

import jax
import jax.numpy as jnp
from jax import lax
from jax.experimental import pallas as pl
from jax.experimental.pallas import tpu as pltpu
from jax.sharding import PartitionSpec as P

ITERS = 3
CHUNK = 8
CENTRE = 7.5
SCALE = 2.5
PANEL = 8
VMEM_BYTES = 24 * 1024 * 1024
MESH = pl.DeviceIdType.MESH


def mm(left, right, left_dim=1, right_dim=0):
    return lax.dot_general(
        left,
        right,
        (((left_dim,), (right_dim,)), ((), ())),
        precision=lax.Precision.HIGHEST,
        preferred_element_type=jnp.float32,
    )


def factor(matrix):
    size = matrix.shape[0]
    rows = lax.broadcasted_iota(jnp.int32, (size, size), 0)
    columns = lax.broadcasted_iota(jnp.int32, (size, size), 1)
    upper = matrix
    inverse = jnp.where(rows == columns, 1.0, 0.0).astype(jnp.float32)
    for start in range(0, size, PANEL):
        panel = [
            jnp.broadcast_to(upper[:, start + m : start + m + 1], (size, size)) for m in range(PANEL)
        ]
        for m in range(PANEL):
            at = start + m
            pivot = panel[m][at : at + 1, :]
            root = lax.rsqrt(pivot)
            root = root * (1.5 - 0.5 * pivot * root * root)
            below = jnp.where(rows > at, panel[m] * root, 0.0)
            upper_row = upper[at : at + 1, :] * root
            inverse_row = inverse[at : at + 1, :] * root
            upper = jnp.where(rows == at, upper_row, upper - below * upper_row)
            inverse = jnp.where(rows == at, inverse_row, inverse - below * inverse_row)
            for later in range(m + 1, PANEL):
                panel[later] = panel[later] - below * below[start + later : start + later + 1, :]
    return jnp.where(columns >= rows, upper, 0.0), inverse


def pack(matrix, lanes):
    per = lanes // matrix.shape[1]
    rows = matrix.shape[0] // per
    return jnp.concatenate([matrix[i * rows : (i + 1) * rows] for i in range(per)], axis=1)


def unpack(packed, size):
    per = packed.shape[1] // size
    return jnp.concatenate([packed[:, i * size : (i + 1) * size] for i in range(per)], axis=0)


def kernel(
    nx, ny, signs_hbm, diagonal_hbm, alphas_ref, betas_ref, next_ref,
    signs_ref, diagonal_ref, own_ref, fetch, fields, split, part_x, part_y,
    send_halo, recv_halo, send_x, recv_x, send_y, recv_y,
):
    planes, lines, lanes = diagonal_ref.shape
    cells = planes * lines
    probes = signs_ref.shape[0] // cells
    chunks = probes // CHUNK
    gx, gy = lax.axis_index("gx"), lax.axis_index("gy")

    def x_device(offset):
        return lax.rem(gx + offset, nx)

    def y_device(offset):
        return lax.rem(gy + offset, ny)

    fetches = (
        pltpu.make_async_copy(signs_hbm, signs_ref, fetch.at[0]),
        pltpu.make_async_copy(diagonal_hbm, diagonal_ref, fetch.at[1]),
    )
    for copy in fetches:
        copy.start()
    barrier = pltpu.get_barrier_semaphore()
    for offset in range(1, nx):
        pl.semaphore_signal(barrier, inc=1, device_id={"gx": x_device(offset)}, device_id_type=MESH)
    for offset in range(1, ny):
        pl.semaphore_signal(barrier, inc=1, device_id={"gy": y_device(offset)}, device_id_type=MESH)

    inner_x, inner_y = pl.ds(1, planes), pl.ds(1, lines)

    def halo_copies(step):
        here = fields.at[step]
        moves = (
            (here.at[planes, inner_y], here.at[0, inner_y], {"gx": x_device(1)}),
            (here.at[1, inner_y], here.at[planes + 1, inner_y], {"gx": x_device(nx - 1)}),
            (here.at[inner_x, lines], here.at[inner_x, 0], {"gy": y_device(1)}),
            (here.at[inner_x, 1], here.at[inner_x, lines + 1], {"gy": y_device(ny - 1)}),
        )
        return [
            pltpu.make_async_remote_copy(
                src_ref=source,
                dst_ref=target,
                send_sem=send_halo.at[step, side],
                recv_sem=recv_halo.at[step, side],
                device_id=device,
                device_id_type=MESH,
            )
            for side, (source, target, device) in enumerate(moves)
        ]

    def load_chunk(chunk):
        for x in range(planes):
            for y in range(lines):
                start = chunk * CHUNK * cells + x * lines + y
                bits = signs_ref[pl.ds(start, CHUNK, stride=cells), :]
                fields[chunk, x + 1, y + 1] = 2.0 * bits.astype(jnp.float32) - 1.0

    for copy in fetches:
        copy.wait()
    load_chunk(0)
    for x in range(planes):
        for y in range(lines):
            own = (diagonal_ref[x, y : y + 1, :] + (6.0 - CENTRE)) * (1.0 / SCALE)
            own_ref[x, y] = jnp.broadcast_to(own, (CHUNK, lanes))
    pl.semaphore_wait(barrier, nx + ny - 2)
    for chunk in range(chunks):
        if chunk > 0:
            load_chunk(chunk)
        for copy in halo_copies(chunk):
            copy.start()

    def split_level(level):
        for x in range(planes):
            for y in range(lines):
                value = jnp.concatenate(
                    [fields[level * chunks + c, x + 1, y + 1] for c in range(chunks)], axis=0
                )
                high = value.astype(jnp.bfloat16)
                low = (value - high.astype(jnp.float32)).astype(jnp.bfloat16)
                at = pl.ds((x * lines + y) * lanes, lanes)
                split[level, 0:probes, at] = high
                split[level, probes : 2 * probes, at] = low

    def gram(left, right):
        product = lax.dot_general(
            split[left], split[right], (((1,), (1,)), ((), ())), preferred_element_type=jnp.float32
        )
        return (
            (product[probes:, probes:] + (product[:probes, probes:] + product[probes:, :probes]))
            + product[:probes, :probes]
        )

    height = part_x.shape[2] // 2

    def along(group, count, offset, part, send, recv, me, device):
        rows = pl.ds(0, height * count)
        return pltpu.make_async_remote_copy(
            src_ref=part.at[group, me, rows],
            dst_ref=part.at[group, me, rows],
            send_sem=send.at[group, offset],
            recv_sem=recv.at[group, offset],
            device_id=device,
            device_id_type=MESH,
        )

    def x_copies(group, count):
        return [
            along(group, count, o, part_x, send_x, recv_x, gx, {"gx": x_device(o)})
            for o in range(1, nx)
        ]

    def y_copies(group, count):
        return [
            along(group, count, o, part_y, send_y, recv_y, gy, {"gy": y_device(o)})
            for o in range(1, ny)
        ]

    def begin(group, matrices):
        for i, matrix in enumerate(matrices):
            part_x[group, gx, i * height : (i + 1) * height] = pack(matrix, lanes)
        for copy in x_copies(group, len(matrices)):
            copy.start()

    def added(part, group, count, slots):
        value = part[group, 0, 0 : height * count]
        for slot in range(1, slots):
            value = value + part[group, slot, 0 : height * count]
        return value

    def middle(group, count):
        for copy in x_copies(group, count):
            copy.wait_recv()
        part_y[group, gy, 0 : height * count] = added(part_x, group, count, nx)
        for copy in y_copies(group, count):
            copy.start()

    def end(group, count):
        for copy in y_copies(group, count):
            copy.wait_recv()
        value = added(part_y, group, count, ny)
        return [unpack(value[i * height : (i + 1) * height], probes) for i in range(count)]

    def apply_level(level, first=0, last=None):
        def apply_chunk(chunk, carry):
            step = level * chunks + chunk
            for copy in halo_copies(step):
                copy.wait_recv()
            before_line = [fields[step, x, 0] for x in range(1, planes + 1)]
            line = [fields[step, x, 1] for x in range(1, planes + 1)]
            for y in range(1, lines + 1):
                after_line = [fields[step, x, y + 1] for x in range(1, planes + 1)]
                row = [fields[step, 0, y]] + line + [fields[step, planes + 1, y]]
                for x in range(1, planes + 1):
                    value = row[x]
                    beside = row[x - 1] + row[x + 1]
                    beside = beside + (before_line[x - 1] + after_line[x - 1])
                    beside = beside + (pltpu.roll(value, 1, 1) + pltpu.roll(value, lanes - 1, 1))
                    fields[step + chunks, x, y] = (
                        own_ref[x - 1, y - 1] * value - beside * (1.0 / SCALE)
                    )
                before_line, line = line, after_line
            if level + 1 < ITERS:
                for copy in halo_copies(step + chunks):
                    copy.start()
            return carry

        lax.fori_loop(first, chunks if last is None else last, apply_chunk, 0)

    levels = ITERS + 1
    moment = []
    lower, inverse_of = {}, {}
    uppers, inverses, before = [], [], []
    rows = lax.broadcasted_iota(jnp.int32, (probes, probes), 0)
    columns = lax.broadcasted_iota(jnp.int32, (probes, probes), 1)
    shift = jnp.where(rows == columns, CENTRE, 0.0).astype(jnp.float32)

    def schur(k, j, matrix):
        for i in range(j):
            matrix = matrix - mm(lower[k, i], lower[j, i], 1, 1)
        return matrix

    def factor_level(j):
        upper, inverse = factor(schur(j, j, moment[2 * j]))
        uppers.append(upper)
        inverses.append(inverse)

    def link(k, j):
        lower[k, j] = mm(schur(k, j, moment[j + k]), inverses[j], 1, 1)

    def coefficients(j):
        inside = lower[j + 1, j]
        if j > 0:
            inside = inside - mm(lower[j, j - 1], before[j - 1], 1, 1)
        alphas_ref[j] = shift + SCALE * mm(inverses[j], inside)

    def coupling(j):
        before.append(mm(uppers[j + 1], inverses[j], 1, 1))
        betas_ref[j] = SCALE * before[j]

    def invert_row(j):
        inverse_of[j, j] = inverses[j]
        for k in range(j):
            gathered = mm(lower[j, k], inverse_of[k, k])
            for i in range(k + 1, j):
                gathered = gathered + mm(lower[j, i], inverse_of[i, k])
            inverse_of[j, k] = -mm(inverses[j], gathered)

    split_level(0)
    begin(0, [gram(0, 0)])
    apply_level(0)
    split_level(1)
    begin(1, [gram(0, 1), gram(1, 1)])
    middle(0, 1)
    apply_level(1)
    split_level(2)
    begin(2, [gram(1, 2), gram(2, 2)])
    middle(1, 2)
    moment.extend(end(0, 1))
    factor_level(0)
    apply_level(2)
    middle(2, 2)
    split_level(3)
    begin(3, [gram(2, 3), gram(3, 3)])
    moment.extend(end(1, 2))
    link(1, 0)
    link(2, 0)
    factor_level(1)
    middle(3, 2)
    coefficients(0)
    coupling(0)
    invert_row(0)
    invert_row(1)
    moment.extend(end(2, 2))
    link(3, 0)
    link(2, 1)
    link(3, 1)
    factor_level(2)
    coefficients(1)
    coupling(1)
    invert_row(2)
    known = jnp.concatenate(
        [
            mm(lower[3, 0], inverse_of[0, 0]) + mm(lower[3, 1], inverse_of[1, 0]),
            mm(lower[3, 1], inverse_of[1, 1]),
            jnp.zeros((probes, probes), jnp.float32),
        ],
        axis=1,
    )
    last_row = jnp.concatenate([inverse_of[2, k] for k in range(3)], axis=1)
    known_link = mm(lower[3, 0], lower[2, 0], 1, 1) + mm(lower[3, 1], lower[2, 1], 1, 1)
    known_pivot = mm(lower[3, 0], lower[3, 0], 1, 1) + mm(lower[3, 1], lower[3, 1], 1, 1)
    known_inside = mm(lower[2, 1], before[1], 1, 1)
    odd, even = end(3, 2)
    lower[3, 2] = mm(odd - known_link, inverses[2], 1, 1)
    upper, inverse = factor((even - known_pivot) - mm(lower[3, 2], lower[3, 2], 1, 1))
    mixed = -mm(inverse, known + mm(lower[3, 2], last_row))
    mixing = [mixed[:, k * probes : (k + 1) * probes] for k in range(3)] + [inverse]
    alphas_ref[2] = shift + SCALE * mm(inverses[2], lower[3, 2] - known_inside)
    betas_ref[2] = SCALE * mm(upper, inverses[2], 1, 1)

    pieces = []
    for block in mixing:
        high = block.astype(jnp.bfloat16)
        pieces.append((high, (block - high.astype(jnp.float32)).astype(jnp.bfloat16)))
    weights = jnp.concatenate(
        [jnp.concatenate([part[side] for part in pieces for _ in range(2)], axis=1) for side in range(2)],
        axis=0,
    )
    group = 4
    basis = split.at[...].reshape(levels * 2 * probes, split.shape[2])
    for start in range(0, cells, group):
        product = jnp.dot(
            weights,
            basis[:, start * lanes : (start + group) * lanes],
            preferred_element_type=jnp.float32,
        )
        product = product[:probes] + product[probes:]
        for inner in range(group):
            next_ref[pl.ds(start + inner, probes, stride=cells), :] = product[
                :, inner * lanes : (inner + 1) * lanes
            ]

    def finish(step, carry):
        for copy in halo_copies(step):
            copy.wait_send()
        return carry

    lax.fori_loop(0, ITERS * chunks, finish, 0)
    for index, count in enumerate((1, 2, 2, 2)):
        for copy in x_copies(index, count) + y_copies(index, count):
            copy.wait_send()


def emit(alphas_ref, betas_ref, next_ref, alphas_out, betas_out, next_out, sems):
    moves = ((next_ref, next_out), (alphas_ref, alphas_out), (betas_ref, betas_out))
    copies = [pltpu.make_async_copy(a, b, sems.at[i]) for i, (a, b) in enumerate(moves)]
    for copy in copies:
        copy.start()
    for copy in copies:
        copy.wait()


def per_device(nx, ny, probe_signs, diagonal):
    probes, planes, lines, lanes = probe_signs.shape
    chunks = probes // CHUNK
    levels = ITERS + 1
    height = probes * probes // lanes
    cells = planes * lines
    small = jax.ShapeDtypeStruct((ITERS, probes, probes), jnp.float32)
    vmem = pl.BlockSpec(memory_space=pltpu.VMEM)
    hbm = pl.BlockSpec(memory_space=pltpu.HBM)
    dma = pltpu.SemaphoreType.DMA
    full = jax.ShapeDtypeStruct((probes * cells, lanes), jnp.float32)
    alphas, betas, block = pl.pallas_call(
        functools.partial(kernel, nx, ny),
        out_shape=(small, small, full),
        in_specs=[hbm, hbm],
        out_specs=(vmem, vmem, vmem),
        scratch_shapes=[
            pltpu.VMEM((probes * cells, lanes), jnp.int32),
            pltpu.VMEM(diagonal.shape, jnp.float32),
            pltpu.VMEM((planes, lines, CHUNK, lanes), jnp.float32),
            dma((2,)),
            pltpu.VMEM((levels * chunks, planes + 2, lines + 2, CHUNK, lanes), jnp.float32),
            pltpu.VMEM((levels, 2 * probes, cells * lanes), jnp.bfloat16),
            pltpu.VMEM((levels, nx, 2 * height, lanes), jnp.float32),
            pltpu.VMEM((levels, ny, 2 * height, lanes), jnp.float32),
            dma((ITERS * chunks, 4)),
            dma((ITERS * chunks, 4)),
            dma((levels, nx)),
            dma((levels, nx)),
            dma((levels, ny)),
            dma((levels, ny)),
        ],
        compiler_params=pltpu.CompilerParams(
            collective_id=0, has_side_effects=True, vmem_limit_bytes=VMEM_BYTES
        ),
        name="lanczos",
    )(
        pltpu.with_memory_space_constraint(probe_signs.reshape(probes * cells, lanes), pltpu.HBM),
        pltpu.with_memory_space_constraint(diagonal, pltpu.HBM),
    )
    alphas, betas, block = pl.pallas_call(
        emit,
        out_shape=(small, small, full),
        in_specs=[vmem] * 3,
        out_specs=(hbm,) * 3,
        scratch_shapes=[dma((3,))],
        compiler_params=pltpu.CompilerParams(vmem_limit_bytes=VMEM_BYTES),
        name="emit",
    )(alphas, betas, block)
    return alphas, betas, block.reshape(probes, planes, lines, lanes)


def solution(mesh):
    nx, ny = mesh.shape["gx"], mesh.shape["gy"]
    in_specs = (P(None, "gx", "gy", None), P("gx", "gy", None))
    out_specs = (P(), P(), P(None, "gx", "gy", None))
    return jax.shard_map(
        functools.partial(per_device, nx, ny),
        mesh=mesh,
        in_specs=in_specs,
        out_specs=out_specs,
        check_vma=False,
    )
```

```python
import functools

import jax
import jax.numpy as jnp
from jax import lax
from jax.experimental import pallas as pl
from jax.experimental.pallas import tpu as pltpu
from jax.sharding import PartitionSpec as P

ITERS = 3
CHUNK = 8
CENTRE = 7.5
SCALE = 2.5
PANEL = 8
VMEM_BYTES = 24 * 1024 * 1024
MESH = pl.DeviceIdType.MESH


def mm(left, right, left_dim=1, right_dim=0):
    return lax.dot_general(
        left,
        right,
        (((left_dim,), (right_dim,)), ((), ())),
        precision=lax.Precision.HIGHEST,
        preferred_element_type=jnp.float32,
    )


def factor(matrix):
    size = matrix.shape[0]
    rows = lax.broadcasted_iota(jnp.int32, (size, size), 0)
    columns = lax.broadcasted_iota(jnp.int32, (size, size), 1)
    upper = matrix
    inverse = jnp.where(rows == columns, 1.0, 0.0).astype(jnp.float32)
    for start in range(0, size, PANEL):
        panel = [
            jnp.broadcast_to(upper[:, start + m : start + m + 1], (size, size)) for m in range(PANEL)
        ]
        for m in range(PANEL):
            at = start + m
            pivot = panel[m][at : at + 1, :]
            root = lax.rsqrt(pivot)
            root = root * (1.5 - 0.5 * pivot * root * root)
            below = jnp.where(rows > at, panel[m] * root, 0.0)
            upper_row = upper[at : at + 1, :] * root
            inverse_row = inverse[at : at + 1, :] * root
            upper = jnp.where(rows == at, upper_row, upper - below * upper_row)
            inverse = jnp.where(rows == at, inverse_row, inverse - below * inverse_row)
            for later in range(m + 1, PANEL):
                panel[later] = panel[later] - below * below[start + later : start + later + 1, :]
    return jnp.where(columns >= rows, upper, 0.0), inverse


def pack(matrix, lanes):
    per = lanes // matrix.shape[1]
    rows = matrix.shape[0] // per
    return jnp.concatenate([matrix[i * rows : (i + 1) * rows] for i in range(per)], axis=1)


def unpack(packed, size):
    per = packed.shape[1] // size
    return jnp.concatenate([packed[:, i * size : (i + 1) * size] for i in range(per)], axis=0)


def kernel(
    nx, ny, signs_hbm, diagonal_hbm, alphas_ref, betas_ref, next_ref,
    signs_ref, diagonal_ref, own_ref, fetch, fields, split, part_x, part_y,
    send_halo, recv_halo, send_x, recv_x, send_y, recv_y,
):
    planes, lines, lanes = diagonal_ref.shape
    cells = planes * lines
    probes = signs_ref.shape[0] // cells
    chunks = probes // CHUNK
    gx, gy = lax.axis_index("gx"), lax.axis_index("gy")

    def x_device(offset):
        return lax.rem(gx + offset, nx)

    def y_device(offset):
        return lax.rem(gy + offset, ny)

    fetches = (
        pltpu.make_async_copy(signs_hbm, signs_ref, fetch.at[0]),
        pltpu.make_async_copy(diagonal_hbm, diagonal_ref, fetch.at[1]),
    )
    for copy in fetches:
        copy.start()
    barrier = pltpu.get_barrier_semaphore()
    for offset in range(1, nx):
        pl.semaphore_signal(barrier, inc=1, device_id={"gx": x_device(offset)}, device_id_type=MESH)
    for offset in range(1, ny):
        pl.semaphore_signal(barrier, inc=1, device_id={"gy": y_device(offset)}, device_id_type=MESH)

    inner_x, inner_y = pl.ds(1, planes), pl.ds(1, lines)

    def halo_copies(step):
        here = fields.at[step]
        moves = (
            (here.at[planes, inner_y], here.at[0, inner_y], {"gx": x_device(1)}),
            (here.at[1, inner_y], here.at[planes + 1, inner_y], {"gx": x_device(nx - 1)}),
            (here.at[inner_x, lines], here.at[inner_x, 0], {"gy": y_device(1)}),
            (here.at[inner_x, 1], here.at[inner_x, lines + 1], {"gy": y_device(ny - 1)}),
        )
        return [
            pltpu.make_async_remote_copy(
                src_ref=source,
                dst_ref=target,
                send_sem=send_halo.at[step, side],
                recv_sem=recv_halo.at[step, side],
                device_id=device,
                device_id_type=MESH,
            )
            for side, (source, target, device) in enumerate(moves)
        ]

    def load_chunk(chunk):
        for x in range(planes):
            for y in range(lines):
                start = chunk * CHUNK * cells + x * lines + y
                bits = signs_ref[pl.ds(start, CHUNK, stride=cells), :]
                fields[chunk, x + 1, y + 1] = 2.0 * bits.astype(jnp.float32) - 1.0

    for copy in fetches:
        copy.wait()
    load_chunk(0)
    for x in range(planes):
        for y in range(lines):
            own = (diagonal_ref[x, y : y + 1, :] + (6.0 - CENTRE)) * (1.0 / SCALE)
            own_ref[x, y] = jnp.broadcast_to(own, (CHUNK, lanes))
    pl.semaphore_wait(barrier, nx + ny - 2)
    for chunk in range(chunks):
        if chunk > 0:
            load_chunk(chunk)
        for copy in halo_copies(chunk):
            copy.start()

    def split_level(level):
        for x in range(planes):
            for y in range(lines):
                value = jnp.concatenate(
                    [fields[level * chunks + c, x + 1, y + 1] for c in range(chunks)], axis=0
                )
                high = value.astype(jnp.bfloat16)
                low = (value - high.astype(jnp.float32)).astype(jnp.bfloat16)
                at = pl.ds((x * lines + y) * lanes, lanes)
                split[level, 0:probes, at] = high
                split[level, probes : 2 * probes, at] = low

    def gram(left, right):
        product = lax.dot_general(
            split[left], split[right], (((1,), (1,)), ((), ())), preferred_element_type=jnp.float32
        )
        return (
            (product[probes:, probes:] + (product[:probes, probes:] + product[probes:, :probes]))
            + product[:probes, :probes]
        )

    height = part_x.shape[2] // 2

    def along(group, count, offset, part, send, recv, me, device):
        rows = pl.ds(0, height * count)
        return pltpu.make_async_remote_copy(
            src_ref=part.at[group, me, rows],
            dst_ref=part.at[group, me, rows],
            send_sem=send.at[group, offset],
            recv_sem=recv.at[group, offset],
            device_id=device,
            device_id_type=MESH,
        )

    def x_copies(group, count):
        return [
            along(group, count, o, part_x, send_x, recv_x, gx, {"gx": x_device(o)})
            for o in range(1, nx)
        ]

    def y_copies(group, count):
        return [
            along(group, count, o, part_y, send_y, recv_y, gy, {"gy": y_device(o)})
            for o in range(1, ny)
        ]

    def begin(group, matrices):
        for i, matrix in enumerate(matrices):
            part_x[group, gx, i * height : (i + 1) * height] = pack(matrix, lanes)
        for copy in x_copies(group, len(matrices)):
            copy.start()

    def added(part, group, count, slots):
        value = part[group, 0, 0 : height * count]
        for slot in range(1, slots):
            value = value + part[group, slot, 0 : height * count]
        return value

    def middle(group, count):
        for copy in x_copies(group, count):
            copy.wait_recv()
        part_y[group, gy, 0 : height * count] = added(part_x, group, count, nx)
        for copy in y_copies(group, count):
            copy.start()

    def end(group, count):
        for copy in y_copies(group, count):
            copy.wait_recv()
        value = added(part_y, group, count, ny)
        return [unpack(value[i * height : (i + 1) * height], probes) for i in range(count)]

    def apply_level(level, first=0, last=None):
        def apply_chunk(chunk, carry):
            step = level * chunks + chunk
            for copy in halo_copies(step):
                copy.wait_recv()
            before_line = [fields[step, x, 0] for x in range(1, planes + 1)]
            line = [fields[step, x, 1] for x in range(1, planes + 1)]
            for y in range(1, lines + 1):
                after_line = [fields[step, x, y + 1] for x in range(1, planes + 1)]
                row = [fields[step, 0, y]] + line + [fields[step, planes + 1, y]]
                for x in range(1, planes + 1):
                    value = row[x]
                    beside = row[x - 1] + row[x + 1]
                    beside = beside + (before_line[x - 1] + after_line[x - 1])
                    beside = beside + (pltpu.roll(value, 1, 1) + pltpu.roll(value, lanes - 1, 1))
                    fields[step + chunks, x, y] = (
                        own_ref[x - 1, y - 1] * value - beside * (1.0 / SCALE)
                    )
                before_line, line = line, after_line
            if level + 1 < ITERS:
                for copy in halo_copies(step + chunks):
                    copy.start()
            return carry

        lax.fori_loop(first, chunks if last is None else last, apply_chunk, 0)

    levels = ITERS + 1
    moment = []
    lower, inverse_of = {}, {}
    uppers, inverses, before = [], [], []
    rows = lax.broadcasted_iota(jnp.int32, (probes, probes), 0)
    columns = lax.broadcasted_iota(jnp.int32, (probes, probes), 1)
    shift = jnp.where(rows == columns, CENTRE, 0.0).astype(jnp.float32)

    def schur(k, j, matrix):
        for i in range(j):
            matrix = matrix - mm(lower[k, i], lower[j, i], 1, 1)
        return matrix

    def factor_level(j):
        upper, inverse = factor(schur(j, j, moment[2 * j]))
        uppers.append(upper)
        inverses.append(inverse)

    def link(k, j):
        lower[k, j] = mm(schur(k, j, moment[j + k]), inverses[j], 1, 1)

    def coefficients(j):
        inside = lower[j + 1, j]
        if j > 0:
            inside = inside - mm(lower[j, j - 1], before[j - 1], 1, 1)
        alphas_ref[j] = shift + SCALE * mm(inverses[j], inside)

    def coupling(j):
        before.append(mm(uppers[j + 1], inverses[j], 1, 1))
        betas_ref[j] = SCALE * before[j]

    def invert_row(j):
        inverse_of[j, j] = inverses[j]
        for k in range(j):
            gathered = mm(lower[j, k], inverse_of[k, k])
            for i in range(k + 1, j):
                gathered = gathered + mm(lower[j, i], inverse_of[i, k])
            inverse_of[j, k] = -mm(inverses[j], gathered)

    split_level(0)
    begin(0, [gram(0, 0)])
    apply_level(0)
    split_level(1)
    begin(1, [gram(0, 1), gram(1, 1)])
    middle(0, 1)
    apply_level(1)
    split_level(2)
    begin(2, [gram(1, 2), gram(2, 2)])
    middle(1, 2)
    moment.extend(end(0, 1))
    factor_level(0)
    apply_level(2)
    split_level(3)
    begin(3, [gram(2, 3), gram(3, 3)])
    middle(2, 2)
    moment.extend(end(1, 2))
    link(1, 0)
    link(2, 0)
    factor_level(1)
    middle(3, 2)
    coefficients(0)
    coupling(0)
    invert_row(0)
    invert_row(1)
    moment.extend(end(2, 2))
    link(3, 0)
    link(2, 1)
    link(3, 1)
    factor_level(2)
    coefficients(1)
    coupling(1)
    invert_row(2)
    known = jnp.concatenate(
        [
            mm(lower[3, 0], inverse_of[0, 0]) + mm(lower[3, 1], inverse_of[1, 0]),
            mm(lower[3, 1], inverse_of[1, 1]),
            jnp.zeros((probes, probes), jnp.float32),
        ],
        axis=1,
    )
    last_row = jnp.concatenate([inverse_of[2, k] for k in range(3)], axis=1)
    known_link = mm(lower[3, 0], lower[2, 0], 1, 1) + mm(lower[3, 1], lower[2, 1], 1, 1)
    known_pivot = mm(lower[3, 0], lower[3, 0], 1, 1) + mm(lower[3, 1], lower[3, 1], 1, 1)
    known_inside = mm(lower[2, 1], before[1], 1, 1)
    odd, even = end(3, 2)
    lower[3, 2] = mm(odd - known_link, inverses[2], 1, 1)
    upper, inverse = factor((even - known_pivot) - mm(lower[3, 2], lower[3, 2], 1, 1))
    mixed = -mm(inverse, known + mm(lower[3, 2], last_row))
    mixing = [mixed[:, k * probes : (k + 1) * probes] for k in range(3)] + [inverse]
    alphas_ref[2] = shift + SCALE * mm(inverses[2], lower[3, 2] - known_inside)
    betas_ref[2] = SCALE * mm(upper, inverses[2], 1, 1)

    pieces = []
    for block in mixing:
        high = block.astype(jnp.bfloat16)
        pieces.append((high, (block - high.astype(jnp.float32)).astype(jnp.bfloat16)))
    weights = jnp.concatenate(
        [jnp.concatenate([part[side] for part in pieces for _ in range(2)], axis=1) for side in range(2)],
        axis=0,
    )
    group = 4
    basis = split.at[...].reshape(levels * 2 * probes, split.shape[2])
    for start in range(0, cells, group):
        product = jnp.dot(
            weights,
            basis[:, start * lanes : (start + group) * lanes],
            preferred_element_type=jnp.float32,
        )
        product = product[:probes] + product[probes:]
        for inner in range(group):
            next_ref[pl.ds(start + inner, probes, stride=cells), :] = product[
                :, inner * lanes : (inner + 1) * lanes
            ]

    def finish(step, carry):
        for copy in halo_copies(step):
            copy.wait_send()
        return carry

    lax.fori_loop(0, ITERS * chunks, finish, 0)
    for index, count in enumerate((1, 2, 2, 2)):
        for copy in x_copies(index, count) + y_copies(index, count):
            copy.wait_send()


def emit(alphas_ref, betas_ref, next_ref, alphas_out, betas_out, next_out, sems):
    moves = ((next_ref, next_out), (alphas_ref, alphas_out), (betas_ref, betas_out))
    copies = [pltpu.make_async_copy(a, b, sems.at[i]) for i, (a, b) in enumerate(moves)]
    for copy in copies:
        copy.start()
    for copy in copies:
        copy.wait()


def per_device(nx, ny, probe_signs, diagonal):
    probes, planes, lines, lanes = probe_signs.shape
    chunks = probes // CHUNK
    levels = ITERS + 1
    height = probes * probes // lanes
    cells = planes * lines
    small = jax.ShapeDtypeStruct((ITERS, probes, probes), jnp.float32)
    vmem = pl.BlockSpec(memory_space=pltpu.VMEM)
    hbm = pl.BlockSpec(memory_space=pltpu.HBM)
    dma = pltpu.SemaphoreType.DMA
    full = jax.ShapeDtypeStruct((probes * cells, lanes), jnp.float32)
    alphas, betas, block = pl.pallas_call(
        functools.partial(kernel, nx, ny),
        out_shape=(small, small, full),
        in_specs=[hbm, hbm],
        out_specs=(vmem, vmem, vmem),
        scratch_shapes=[
            pltpu.VMEM((probes * cells, lanes), jnp.int32),
            pltpu.VMEM(diagonal.shape, jnp.float32),
            pltpu.VMEM((planes, lines, CHUNK, lanes), jnp.float32),
            dma((2,)),
            pltpu.VMEM((levels * chunks, planes + 2, lines + 2, CHUNK, lanes), jnp.float32),
            pltpu.VMEM((levels, 2 * probes, cells * lanes), jnp.bfloat16),
            pltpu.VMEM((levels, nx, 2 * height, lanes), jnp.float32),
            pltpu.VMEM((levels, ny, 2 * height, lanes), jnp.float32),
            dma((ITERS * chunks, 4)),
            dma((ITERS * chunks, 4)),
            dma((levels, nx)),
            dma((levels, nx)),
            dma((levels, ny)),
            dma((levels, ny)),
        ],
        compiler_params=pltpu.CompilerParams(
            collective_id=0, has_side_effects=True, vmem_limit_bytes=VMEM_BYTES
        ),
        name="lanczos",
    )(
        pltpu.with_memory_space_constraint(probe_signs.reshape(probes * cells, lanes), pltpu.HBM),
        pltpu.with_memory_space_constraint(diagonal, pltpu.HBM),
    )
    alphas, betas, block = pl.pallas_call(
        emit,
        out_shape=(small, small, full),
        in_specs=[vmem] * 3,
        out_specs=(hbm,) * 3,
        scratch_shapes=[dma((3,))],
        compiler_params=pltpu.CompilerParams(vmem_limit_bytes=VMEM_BYTES),
        name="emit",
    )(alphas, betas, block)
    return alphas, betas, block.reshape(probes, planes, lines, lanes)


def solution(mesh):
    nx, ny = mesh.shape["gx"], mesh.shape["gy"]
    in_specs = (P(None, "gx", "gy", None), P("gx", "gy", None))
    out_specs = (P(), P(), P(None, "gx", "gy", None))
    return jax.shard_map(
        functools.partial(per_device, nx, ny),
        mesh=mesh,
        in_specs=in_specs,
        out_specs=out_specs,
        check_vma=False,
    )
```
